32 devices in a mesh: row: 4 (over z), col: 4 (over y, x), layer: 2 (over core).
Axes of the slice: x: 2, y: 2, z: 4, core: 2. Of those that a mesh axis runs over, the one named last changes fastest.
Arguments:
- coeffs: bfloat16 [8192, 4096], P('row', 'col'), may hold values from -6 to 6
- block_sizes: int32 [64], P('row'), may hold values from 64 to 128, as said below
- neighbours: int32 [64, 16], P('row'), may hold values from 0 to 63, as said below
- ham_blocks: bfloat16 [64, 16, 128, 128], P('row', 'layer'), may hold values from -0.125 to 0.125
- ovl_blocks: bfloat16 [64, 16, 128, 128], P('row', 'layer'), may hold values from -0.125 to 0.125
Outputs:
- residual: float32 [8192, 4096], P(('row', 'layer'), 'col')
The draws below stay inside these ranges and needn't reach their ends.
Inputs may be any that keep to these rules, and one draw needn't show every extreme that they name: `block_sizes`: some block has exactly 128 live basis functions. `neighbours`: every entry names a block at most 16 blocks from its row's block; slot 0 names the row's own block.
All inputs are finite; a program needn't handle non-finite values.
Results may differ from the reference program's by a relative error of at most 0.0031.
Values may be sent and summed in bfloat16 or wider, within the bound.
No kernel may reach another device: no remote copies, remote signals or barrier semaphores. Data moves between devices by JAX's collectives and lax.ppermute only.
A program may use at most 128 MiB of HBM per device.

```python
import jax
import jax.numpy as jnp
from jax import lax

B = 128
NOCC = 4096
K = 16
NBR = 16
NB = 64
ROWS = 8192


def draw_block_sizes(key, part):
    sizes = jax.random.randint(key, (NB,), B // 2, B + 1).astype(jnp.int32)
    where = jax.random.randint(jax.random.fold_in(key, 7), (), 0, NB)
    return sizes.at[where].set(B).astype(jnp.int32)


def draw_neighbours(key, part):
    offsets = jax.random.randint(key, (NB, K), -NBR, NBR + 1)
    own = jnp.arange(NB, dtype=jnp.int32)
    picked = jnp.clip(own[:, None] + offsets, 0, NB - 1)
    return picked.at[:, 0].set(own).astype(jnp.int32)


def block_scale(stream_key, dims, shards, smallest, largest):
    loudness = 1.0
    for position, blocks in shards:
        steps = jax.random.uniform(jax.random.fold_in(jax.random.fold_in(stream_key, 6), position), (blocks,), jnp.float32, smallest / len(shards), largest / len(shards))
        loudness = loudness * jnp.repeat(jnp.exp(steps), dims[position] // blocks).reshape((-1,) + (1,) * (len(dims) - 1 - position))
    return loudness


def centred(stream_key, dims, width, reach, shards=(), kind=jnp.bfloat16):
    gain = block_scale(stream_key, dims, shards, -0.22, 0.18) if shards else 1.0
    entries = jax.random.normal(stream_key, dims, jnp.float32) * width * gain
    return jnp.minimum(jnp.maximum(entries, -reach), reach).astype(kind)


def setup_inputs(seed: int = 0) -> dict:
    arg_keys = jax.random.split(jax.random.key(seed), 6)
    coeffs = centred(arg_keys[0], (ROWS, NOCC), 1.0, 6.0, ((0, 4), (1, 4)))
    block_sizes = draw_block_sizes(jax.random.fold_in(arg_keys[5], 71), 0)
    neighbours = draw_neighbours(jax.random.fold_in(arg_keys[5], 71), 0)
    ham_blocks = centred(arg_keys[3], (NB, K, B, B), (K * B) ** -0.5, 0.125, ((0, 4), (1, 2)))
    ovl_blocks = centred(arg_keys[4], (NB, K, B, B), (K * B) ** -0.5, 0.125, ((0, 4), (1, 2)))
    return dict(coeffs=coeffs, block_sizes=block_sizes, neighbours=neighbours, ham_blocks=ham_blocks, ovl_blocks=ovl_blocks)


def reference(coeffs, block_sizes, neighbours, ham_blocks, ovl_blocks):
    count_blocks = block_sizes.shape[0]
    block_rows = ham_blocks.shape[2]
    live = (jnp.arange(block_rows, dtype=jnp.int32)[None, :] < block_sizes[:, None])
    cblocks = coeffs.reshape(count_blocks, block_rows, -1) * live[:, :, None].astype(coeffs.dtype)

    def one_row(items):
        hrow, srow, nrow, lrow = items
        picked = cblocks[nrow].astype(jnp.float32)
        wpart = jnp.einsum('kpq,kqn->pn', hrow.astype(jnp.float32), picked) * lrow[:, None]
        vpart = jnp.einsum('kpq,kqn->pn', srow.astype(jnp.float32), picked) * lrow[:, None]
        return wpart.astype(jnp.bfloat16), vpart.astype(jnp.bfloat16)

    hc, sc = lax.map(one_row, (ham_blocks, ovl_blocks, neighbours, live.astype(jnp.float32)))
    total_rows = count_blocks * block_rows
    hc = hc.reshape(total_rows, -1)
    sc = sc.reshape(total_rows, -1)
    masked = cblocks.reshape(total_rows, -1)
    gram = (jnp.dot(masked.T, hc, preferred_element_type=jnp.float32) / total_rows).astype(jnp.bfloat16)
    return hc.astype(jnp.float32) - jnp.dot(sc, gram, preferred_element_type=jnp.float32)
```

```python
import functools

import jax
import jax.numpy as jnp
from jax import lax
from jax.experimental import pallas as pl
from jax.experimental.pallas import tpu as pltpu
from jax.sharding import PartitionSpec as P

F32 = jnp.float32
BF16 = jnp.bfloat16


def swap(x):
    return lax.ppermute(x, "layer", [(0, 1), (1, 0)])


def split_cols():
    cols = lax.axis_size("col")
    first = max(d for d in range(1, cols + 1) if cols % d == 0 and d * d <= cols)
    return first, cols // first


def shift_first(x, step):
    first, second = split_cols()
    pairs = [(a * second + b, (a + step) % first * second + b) for a in range(first) for b in range(second)]
    return lax.ppermute(x, "col", pairs)


def shift_second(x, step):
    first, second = split_cols()
    pairs = [(a * second + b, a * second + (b + step) % second) for a in range(first) for b in range(second)]
    return lax.ppermute(x, "col", pairs)


def sum_rows(part):
    rows = lax.axis_size("row")
    me = lax.axis_index("row")
    half = rows // 2
    total = part

    def plus(a, b):
        return (a.astype(F32) + b.astype(F32)).astype(BF16)

    for t in range(half - 1):
        got = lax.ppermute(total, "row", [(t, t + 1), (rows - 1 - t, rows - 2 - t)])
        total = plus(total, got)
    if rows > 1:
        got = lax.ppermute(total, "row", [(half - 1, half), (half, half - 1)])
        total = plus(total, got)
    for t in reversed(range(half - 1)):
        got = lax.ppermute(total, "row", [(t + 1, t), (rows - 2 - t, rows - 1 - t)])
        total = jnp.where((me == t) | (me == rows - 1 - t), got, total)
    return total


def spmm_kernel(where, sizes, own, before, after, ham_a, ham_b, ovl_a, ovl_b, hc, sc, held, picked, sems):
    i = pl.program_id(0)
    blocks = pl.num_programs(0)
    slots, depth = ham_a.shape[1], ham_a.shape[2]

    @pl.when(i == 0)
    def _():
        copies = [
            pltpu.make_async_copy(src, held.at[pl.ds(n * blocks, blocks)], sems.at[n])
            for n, src in enumerate((before, own, after))
        ]
        for copy in copies:
            copy.start()
        for copy in copies:
            copy.wait()

    for k in range(2 * slots):
        picked[k * depth : (k + 1) * depth, :] = held[where[i, k]]
    left = jnp.concatenate(
        [
            jnp.concatenate([a[0, k] for a in pair for k in range(slots)], axis=1)
            for pair in ((ham_a, ham_b), (ovl_a, ovl_b))
        ],
        axis=0,
    )
    both = jnp.dot(left, picked[...], preferred_element_type=F32)
    alive = lax.broadcasted_iota(jnp.int32, (depth, 1), 0) < sizes[i]
    hc[...] = jnp.where(alive, both[:depth], 0.0).astype(BF16)
    sc[...] = jnp.where(alive, both[depth:], 0.0).astype(BF16)


def spmm(where, sizes, own, before, after, ham_a, ham_b, ovl_a, ovl_b):
    blocks, slots, depth, _ = ham_a.shape
    rows, cols = own.shape
    own, before, after = (x.reshape(blocks, depth, cols) for x in (own, before, after))
    mats = pl.BlockSpec((1, slots, depth, depth), lambda i, *_: (i, 0, 0, 0))
    anywhere = pl.BlockSpec(memory_space=pl.ANY)
    out = pl.BlockSpec((depth, cols), lambda i, *_: (i, 0))
    return pl.pallas_call(
        spmm_kernel,
        out_shape=[jax.ShapeDtypeStruct((rows, cols), BF16)] * 2,
        grid_spec=pltpu.PrefetchScalarGridSpec(
            num_scalar_prefetch=2,
            grid=(blocks,),
            in_specs=[anywhere] * 3 + [mats] * 4,
            out_specs=[out, out],
            scratch_shapes=[
                pltpu.VMEM((3 * blocks, depth, cols), BF16),
                pltpu.VMEM((2 * slots * depth, cols), BF16),
                pltpu.SemaphoreType.DMA((3,)),
            ],
        ),
        cost_estimate=pl.CostEstimate(
            flops=8 * rows * slots * depth * cols,
            bytes_accessed=8 * blocks * slots * depth * depth + 10 * rows * cols,
            transcendentals=0,
        ),
        name="spmm",
    )(where, sizes, own, before, after, ham_a, ham_b, ovl_a, ovl_b)


def body(coeffs, block_sizes, neighbours, ham_blocks, ovl_blocks):
    blocks, slots, depth, _ = ham_blocks.shape
    rows, cols = coeffs.shape
    devices = lax.axis_size("row")
    first, second = split_cols()
    row_id, layer_id = lax.axis_index("row"), lax.axis_index("layer")
    width = cols // 2
    chunks = 2 if width % 256 == 0 else 1
    piece = width // chunks
    half = rows // 2

    live = jnp.arange(depth, dtype=jnp.int32)[None, :] < block_sizes[:, None]
    mask = live.reshape(rows, 1).astype(coeffs.dtype)
    mine = [
        lax.dynamic_slice_in_dim(coeffs, layer_id * width + j * piece, piece, 1) * mask
        for j in range(chunks)
    ]
    up = [(i, i + 1) for i in range(devices - 1)]
    down = [(j, i) for i, j in up]
    halo = [(lax.ppermute(x, "row", up), lax.ppermute(x, "row", down)) for x in mine]
    ham_other, ovl_other = swap(ham_blocks), swap(ovl_blocks)
    raw = lax.dynamic_slice_in_dim(coeffs, layer_id * width, width, 1)
    sides = [coeffs]
    for step in range(1, first):
        got = shift_first(raw, step)
        both = jnp.zeros_like(coeffs)
        both = lax.dynamic_update_slice(both, got, (0, layer_id * width))
        both = lax.dynamic_update_slice(both, swap(got), (0, (1 - layer_id) * width))
        sides.append(both)
    side = jnp.concatenate(sides, axis=1)

    where = neighbours - (row_id * blocks - blocks)
    where = jnp.where(layer_id == 0, where, jnp.roll(where, slots, axis=1))

    products = [
        spmm(where, block_sizes, x, before, after, ham_blocks, ham_other, ovl_blocks, ovl_other)
        for x, (before, after) in zip(mine, halo)
    ]
    total_rows = rows * devices
    grams = {}
    hcs = {}
    for j, (hc, _) in enumerate(products):
        for s in range(second):
            hcs[j, s] = hc if s == 0 else shift_second(hc, s)
    for j in range(chunks):
        for s in range(second):
            part = lax.dot_general(side, hcs[j, s], (((0,), (0,)), ((), ())), preferred_element_type=F32)
            grams[j, s] = sum_rows((part / total_rows).astype(BF16))

    hc = jnp.concatenate([p[0] for p in products], axis=1)
    sc = jnp.concatenate([p[1] for p in products], axis=1)

    def turn(x):
        keep = lax.dynamic_slice_in_dim(x, layer_id * half, half, 0)
        got = swap(lax.dynamic_slice_in_dim(x, (1 - layer_id) * half, half, 0))
        whole = jnp.zeros((half, cols), x.dtype)
        whole = lax.dynamic_update_slice(whole, keep, (0, layer_id * width))
        return lax.dynamic_update_slice(whole, got, (0, (1 - layer_id) * width))

    hc, sc = turn(hc), turn(sc)
    wide = jnp.concatenate([sc] + [shift_first(sc, step) for step in range(1, first)], axis=1)

    out = []
    for j in range(chunks):
        own = None
        for s in reversed(range(second)):
            g = grams[j, s]
            g2 = jnp.concatenate([g, swap(g)], axis=1)
            prod = jnp.dot(wide, g2, preferred_element_type=F32)
            if s:
                prod = shift_second(prod.astype(BF16), second - s).astype(F32)
            own = prod if own is None else own + prod
        out.append(own)
    mine_first = jnp.concatenate([x[:, :piece] for x in out] + [x[:, piece:] for x in out], axis=1)
    other_first = jnp.concatenate([x[:, piece:] for x in out] + [x[:, :piece] for x in out], axis=1)
    projected = jnp.where(layer_id == 0, mine_first, other_first)
    return hc.astype(F32) - projected


def solution(mesh):
    return jax.shard_map(
        body,
        mesh=mesh,
        in_specs=(
            P("row", "col"),
            P("row"),
            P("row", None),
            P("row", "layer", None, None),
            P("row", "layer", None, None),
        ),
        out_specs=P(("row", "layer"), "col"),
        check_vma=False,
    )
```

```python
import jax
import jax.numpy as jnp
from jax import lax
from jax.experimental import pallas as pl
from jax.experimental.pallas import tpu as pltpu
from jax.sharding import PartitionSpec as P

F32 = jnp.float32
BF16 = jnp.bfloat16
SPMM_VMEM = 28 << 20
VMEM = pl.BlockSpec(memory_space=pltpu.VMEM)
SMEM = pl.BlockSpec(memory_space=pltpu.SMEM)
ANY = pl.BlockSpec(memory_space=pl.ANY)


def near(*arrays):
    return [pltpu.with_memory_space_constraint(x, pltpu.VMEM) for x in arrays]


def after(x, *earlier):
    return lax.optimization_barrier((x, *earlier))[0]


def swap(x):
    return lax.ppermute(x, "layer", [(0, 1), (1, 0)])


def split_cols():
    cols = lax.axis_size("col")
    first = max(d for d in range(1, cols + 1) if cols % d == 0 and d * d <= cols)
    return first, cols // first


def shift_first(x, step):
    first, second = split_cols()
    pairs = [(a * second + b, (a + step) % first * second + b) for a in range(first) for b in range(second)]
    return lax.ppermute(x, "col", pairs)


def shift_cross(x, step):
    first, second = split_cols()
    pairs = [
        ((a * second + b) * 2 + c, ((a + step) % first * second + b) * 2 + 1 - c)
        for a in range(first)
        for b in range(second)
        for c in range(2)
    ]
    return lax.ppermute(x, ("col", "layer"), pairs)


def shift_second(x, step):
    first, second = split_cols()
    pairs = [(a * second + b, a * second + (b + step) % second) for a in range(first) for b in range(second)]
    return lax.ppermute(x, "col", pairs)


def plus(a, b):
    return (a.astype(F32) + b.astype(F32)).astype(BF16)


def spmm(where, sizes, layer, own, before, behind, mats, earlier):
    blocks, slots, depth, _ = mats[0].shape
    rows, cols = own.shape
    past = earlier[0].shape[0] if earlier else 0

    def kernel(where, sizes, layer, own, before, behind, ham_a, ham_b, ovl_a, ovl_b, *refs):
        old, (hc, keep, give_s, give_h, held, *mats, sems, arrived) = refs[:-11], refs[-11:]
        half = blocks // 2
        me = layer[0]
        copies = [
            pltpu.make_async_copy(src, held.at[pl.ds(n * blocks, blocks)], sems.at[n])
            for n, src in enumerate((own, before, behind))
        ]
        for copy in copies:
            copy.start()

        def fetch(row):
            pairs = zip((ham_a, ham_b, ovl_a, ovl_b), mats)
            return [
                pltpu.make_async_copy(src.at[row], dst.at[row], arrived.at[n, row]) for n, (src, dst) in enumerate(pairs)
            ]

        def order(n):
            return me * half + n, (1 - me) * half + n

        def begin(n, carry):
            for row in order(n):
                for copy in fetch(row):
                    copy.start()
            return carry

        lax.fori_loop(0, half, begin, 0)
        for copy in copies:
            copy.wait()
        ham_near, ham_far, ovl_near, ovl_far = mats
        for src, dst in zip(old, (keep, give_s, give_h)):
            dst[:past] = src[...]

        def product(row):
            for copy in fetch(row):
                copy.wait()
            both = None
            for k in range(0, 2 * slots, 2):
                pair = (ham_near, ovl_near) if k < slots else (ham_far, ovl_far)
                left = jnp.concatenate(
                    [jnp.concatenate([m[row, k % slots], m[row, k % slots + 1]], axis=1) for m in pair], axis=0
                )
                right = jnp.concatenate([held[where[row, k]], held[where[row, k + 1]]], axis=0)
                one = jnp.dot(left, right, preferred_element_type=F32)
                both = one if both is None else both + one
            alive = lax.broadcasted_iota(jnp.int32, (depth, 1), 0) < sizes[row]
            h, s = (jnp.where(alive, x, 0.0).astype(BF16) for x in (both[:depth], both[depth:]))
            hc[pl.ds(pl.multiple_of(row * depth, depth), depth), :] = h
            return h, s

        def step(n, carry):
            at = pl.ds(pl.multiple_of(n * depth, depth), depth)
            first, second = order(n)
            _, s = product(first)
            keep[past, at, :] = s
            h, s = product(second)
            give_s[past, at, :] = s
            give_h[past, at, :] = h
            return carry

        lax.fori_loop(0, half, step, 0)

    shaped = [x.reshape(blocks, depth, cols) for x in (own, before, behind)]
    return pl.pallas_call(
        kernel,
        out_shape=[jax.ShapeDtypeStruct((rows, cols), BF16)]
        + [jax.ShapeDtypeStruct((past + 1, rows // 2, cols), BF16)] * 3,
        in_specs=[SMEM] * 3 + [ANY] * 7 + [VMEM] * len(earlier),
        out_specs=[VMEM] * 4,
        scratch_shapes=[pltpu.VMEM((3 * blocks, depth, cols), BF16)]
        + [pltpu.VMEM(m.shape, BF16) for m in mats]
        + [pltpu.SemaphoreType.DMA((3,)), pltpu.SemaphoreType.DMA((4, blocks))],
        compiler_params=pltpu.CompilerParams(vmem_limit_bytes=SPMM_VMEM),
        cost_estimate=pl.CostEstimate(
            flops=8 * rows * slots * depth * cols,
            bytes_accessed=8 * blocks * slots * depth * depth + 10 * rows * cols,
            transcendentals=0,
        ),
        name="spmm",
    )(where, sizes, layer, *shaped, *mats, *near(*earlier))


def gram(total_rows, layer, lefts, right):
    rows, cols = right.shape
    wide = lefts[0].shape[1]
    tile = min(256, wide)

    def kernel(layer, *refs):
        *lefts, right, out = refs
        for a in range(0, wide, tile):
            total = None
            for n, left in enumerate(lefts):
                size = left.shape[0]
                which = layer[0] if n == 0 else 1 - layer[0]
                some = right[...] if size == rows else right[pl.ds(pl.multiple_of(which * size, size), size), :]
                one = lax.dot_general(
                    left[:, a : a + tile], some, (((0,), (0,)), ((), ())), preferred_element_type=F32
                )
                total = one if total is None else total + one
            out[a : a + tile, :] = (total * (1.0 / total_rows)).astype(BF16)

    return pl.pallas_call(
        kernel,
        out_shape=jax.ShapeDtypeStruct((wide, cols), BF16),
        in_specs=[SMEM] + [VMEM] * (len(lefts) + 1),
        out_specs=VMEM,
        compiler_params=pltpu.CompilerParams(vmem_limit_bytes=8 << 20),
        cost_estimate=pl.CostEstimate(
            flops=2 * rows * wide * cols, bytes_accessed=2 * rows * (wide + cols), transcendentals=0
        ),
        name="gram",
    )(layer, *near(*lefts, right))


def product(layer, stacks, grams, tile, put):
    chunks, half, piece = stacks[0].shape
    for r in range(0, half, tile):
        totals = [None, None]
        for n, stack in enumerate(stacks):
            which = layer if n % 2 == 0 else 1 - layer
            for j in range(chunks):
                at = pl.ds(pl.multiple_of(which * (chunks * piece) + j * piece, piece), piece)
                left = stack[j, r : r + tile, :]
                for c in range(2):
                    one = jnp.dot(left, grams[n // 2][c][at, :], preferred_element_type=F32)
                    totals[c] = one if totals[c] is None else totals[c] + one
        put(r, totals)


def foreign(layer, stacks, grams):
    _, half, piece = stacks[0].shape
    tile = min(256, half)
    count = len(stacks)

    def kernel(layer, *refs):
        stacks, pairs, out = refs[:count], refs[count:-1], refs[-1]

        def put(r, totals):
            for c in range(2):
                out[r : r + tile, c * piece : (c + 1) * piece] = totals[c].astype(BF16)

        product(layer[0], stacks, list(zip(pairs[::2], pairs[1::2])), tile, put)

    return pl.pallas_call(
        kernel,
        out_shape=jax.ShapeDtypeStruct((half, 2 * piece), BF16),
        in_specs=[SMEM] + [VMEM] * (2 * count),
        out_specs=VMEM,
        compiler_params=pltpu.CompilerParams(vmem_limit_bytes=8 << 20),
        name="foreign",
    )(layer, *near(*stacks, *[g for pair in grams for g in pair]))


def finish(layer, j, stacks, grams, hc, hc_other, got, out):
    chunks, half, piece = stacks[0].shape
    width = chunks * piece
    tile = min(256, half)
    steps = half // tile
    count, others = len(stacks), len(got)

    def kernel(layer, *refs):
        stacks, pairs = refs[:count], refs[count : 2 * count]
        hc, hc_other = refs[2 * count], refs[2 * count + 1]
        got = refs[2 * count + 2 : 2 * count + 2 + others]
        out, made, sems = refs[-3:]
        me = layer[0]
        copies = []

        def put(r, totals):
            for c in range(2):
                if c == 0:
                    mine = hc[pl.ds(pl.multiple_of(me * half + r, tile), tile), :]
                else:
                    mine = hc_other[j, r : r + tile, :]
                value = mine.astype(F32) - totals[c]
                for g in got:
                    value = value - g[r : r + tile, c * piece : (c + 1) * piece].astype(F32)
                made[c, r : r + tile, :] = value
                which = me if c == 0 else 1 - me
                at = pl.ds(pl.multiple_of(which * width + j * piece, piece), piece)
                copy = pltpu.make_async_copy(
                    made.at[c, pl.ds(r, tile), :], out.at[pl.ds(r, tile), at], sems.at[c, r // tile]
                )
                copy.start()
                copies.append(copy)

        product(me, stacks, list(zip(pairs[::2], pairs[1::2])), tile, put)
        for copy in copies:
            copy.wait()

    operands = [layer, *near(*stacks, *[g for pair in grams for g in pair], hc, hc_other, *got)]
    specs = [SMEM] + [VMEM] * (len(operands) - 1)
    alias = {}
    if out is not None:
        alias = {len(operands): 0}
        operands.append(out)
        specs.append(ANY)
    return pl.pallas_call(
        kernel,
        out_shape=jax.ShapeDtypeStruct((half, 2 * width), F32),
        in_specs=specs,
        out_specs=ANY,
        scratch_shapes=[pltpu.VMEM((2, half, piece), F32), pltpu.SemaphoreType.DMA((2, steps))],
        input_output_aliases=alias,
        compiler_params=pltpu.CompilerParams(vmem_limit_bytes=8 << 20),
        name="finish",
    )(*operands)


def body(coeffs, block_sizes, neighbours, ham_blocks, ovl_blocks):
    blocks, slots, depth, _ = ham_blocks.shape
    rows, cols = coeffs.shape
    devices = lax.axis_size("row")
    first, second = split_cols()
    row_id, layer_id = lax.axis_index("row"), lax.axis_index("layer")
    layer = layer_id.reshape(1).astype(jnp.int32)
    width = cols // 2
    chunks = 2 if width % 256 == 0 else 1
    piece = width // chunks
    half = rows // 2
    middle = devices // 2

    live = jnp.arange(depth, dtype=jnp.int32)[None, :] < block_sizes[:, None]
    mask = live.reshape(rows, 1).astype(coeffs.dtype)
    mine = [
        lax.dynamic_slice_in_dim(coeffs, layer_id * width + j * piece, piece, 1) * mask for j in range(chunks)
    ]
    up = [(i, i + 1) for i in range(devices - 1)]
    down = [(j, i) for i, j in up]
    halo = []
    for j, x in enumerate(mine):
        before = lax.ppermute(x, "row", up)
        behind = lax.ppermute(x, "row", down)
        halo.append((before, behind))
    raw = lax.dynamic_slice_in_dim(after(coeffs, *mine), layer_id * half, half, 0)
    sides = [shift_first(raw, step) for step in range(1, first)]
    ham_other, ovl_other = swap(after(ham_blocks, *mine)), swap(after(ovl_blocks, *mine))
    mats = (ham_blocks, ham_other, ovl_blocks, ovl_other)

    where = neighbours - row_id * blocks
    where = jnp.where(where < 0, where + 2 * blocks, jnp.where(where >= blocks, where + blocks, where))
    where = jnp.where(layer_id == 0, where, jnp.roll(where, slots, axis=1))

    hcs, joined, token = [], [], None
    lefts = [[coeffs]]
    groups = []
    for j in range(chunks):
        there = list(range(1, second))
        groups += [(j, s) for s in ([0] + there if j < chunks - 1 else there + [0])]
    order = [(j, s, t) for j, s in groups for t in range(first)]
    value = {}
    flight = {}

    stages = []
    for t in range(middle - 1):
        stages.append(([(t, t + 1), (devices - 1 - t, devices - 2 - t)], None))
    if devices > 1:
        stages.append(([(middle - 1, middle), (middle, middle - 1)], None))
    for t in reversed(range(middle - 1)):
        stages.append(([(t + 1, t), (devices - 2 - t, devices - 1 - t)], (row_id == t) | (row_id == devices - 1 - t)))

    def launch(n):
        nonlocal token
        j, s, t = order[n]
        right = hcs[j][s] if token is None else after(hcs[j][s], token)
        token = value[n] = gram(rows * devices, layer, lefts[t], right)
        if stages:
            flight[n] = lax.ppermute(value[n], "row", stages[0][0])

    for j in range(chunks):
        x, (before, behind) = mine[j], halo[j]
        if token is not None:
            x = after(x, token)
        hc, *joined = spmm(where, block_sizes, layer, x, before, behind, mats, joined)
        token = hc
        hcs.append([hc] + [shift_second(hc, s) for s in range(1, second)])
        if j == 0:
            if groups[0] == (0, 0):
                launch(0)
            for got in sides:
                got = after(got, token)
                lefts.append([got, swap(got)])
            if groups[0] == (0, 0):
                for t in range(1, first):
                    launch(t)
    launched = first if groups[0] == (0, 0) else 0

    keep, give_s, give_h = joined
    stacks = [keep, swap(give_s)]
    for step in range(1, first):
        stacks += [shift_first(keep, step), shift_cross(give_s, step)]
    hc_other = swap(give_h)

    depth_of = len(stages)
    ready, done, waiting = {}, {}, []
    out = None
    count = len(order)
    for tick in range(count + depth_of):
        while launched < count and launched <= tick:
            launch(launched)
            launched += 1
        for k in range(depth_of):
            n = tick - k
            if not 0 <= n < count:
                continue
            _, take = stages[k]
            got = after(flight[n], token)
            value[n] = plus(value[n], got) if take is None else jnp.where(take, got, value[n])
            token = value[n]
            if k + 1 < depth_of:
                flight[n] = lax.ppermute(value[n], "row", stages[k + 1][0])
        n = tick - max(depth_of - 1, 0)
        if 0 <= n < count:
            j, s, t = order[n]
            ready[j, s, t] = (value[n], swap(value[n]))
            if t == first - 1:
                waiting.append((j, s))
        while launched < count and launched <= tick + 2 and tick + 1 < count:
            launch(launched)
            launched += 1
        for j, s in list(waiting):
            if s == 0 and any((j, m) not in done for m in range(1, second)):
                continue
            grams = [ready[j, s, t] for t in range(first)]
            mine_first = [after(stacks[0], token)] + stacks[1:]
            if s:
                token = foreign(layer, mine_first, grams)
                done[j, s] = shift_second(token, second - s)
            else:
                got = [done[j, m] for m in range(1, second)]
                token = out = finish(layer, j, mine_first, grams, hcs[j][0], hc_other, got, out)
            waiting.remove((j, s))
    return out


def solution(mesh):
    return jax.shard_map(
        body,
        mesh=mesh,
        in_specs=(
            P("row", "col"),
            P("row"),
            P("row", None),
            P("row", "layer", None, None),
            P("row", "layer", None, None),
        ),
        out_specs=P(("row", "layer"), "col"),
        check_vma=False,
    )
```
